32 devices in a mesh: stn: 4 (over x, core), chan: 8 (over z, y).
Axes of the slice: x: 2, y: 2, z: 4, core: 2. Of those that a mesh axis runs over, the one named last changes fastest.
Arguments:
- voltages: bfloat16 [2, 96, 1024, 256], P(None, None, ('stn', 'chan')), may hold values from -6 to 6
- flagged_ids: int32 [32], replicated, may hold values from 0 to 95, as said below
- work_plan: int32 [4, 8, 2], replicated, may hold values from 8 to 87, as said below
Outputs:
- visibility: bfloat16 [96, 2, 1024, 1024], P('stn', None, 'chan')
- slot_power: float32 [4, 8, 2], P('stn', 'chan')
The draws below stay inside these ranges and needn't reach their ends.
Inputs may be any that keep to these rules, and one draw needn't show every extreme that they name: `flagged_ids`: the flagged channels with stn group a (channels a * 24 to a * 24 + 23) are one contiguous run of 8 channels inside that group; in the first group the run starts at the group's first channel, in the last group it ends at the group's last channel, in the others its position is drawn for each group; the list is ascending. work_plan[a] lists every unflagged channel of group a exactly once, so it holds only channels of that group.
All inputs are finite; a program needn't handle non-finite values.
Results may differ from the reference program's by a relative error of at most 0.001.
Values may be sent and summed in bfloat16 or wider, within the bound.
A program may use at most 128 MiB of HBM per device.

```python
import jax
import jax.numpy as jnp
from jax import lax

S = 1024
TIME = 256
CH_DEV = 3
C = 96
SLOTS = 2
N_STN = 4
N_CHAN = 8


def plan_tables(key):
    group_size = CH_DEV * N_CHAN
    offsets = jax.random.randint(jax.random.fold_in(key, 11), (N_STN,), 0, group_size - N_CHAN + 1).astype(jnp.int32)
    offsets = offsets.at[0].set(0).at[N_STN - 1].set(group_size - N_CHAN)
    starts = jnp.arange(N_STN, dtype=jnp.int32) * group_size
    flagged = (starts + offsets)[:, None] + jnp.arange(N_CHAN, dtype=jnp.int32)[None, :]
    unused_rank = jnp.arange(group_size - N_CHAN, dtype=jnp.int32)
    channels = jnp.where(unused_rank[None, :] < offsets[:, None], unused_rank[None, :], unused_rank[None, :] + N_CHAN) + starts[:, None]
    subkeys = jax.random.split(jax.random.fold_in(key, 12), N_STN)
    orders = jax.vmap(lambda sub_key: jax.random.permutation(sub_key, group_size - N_CHAN))(subkeys)
    table = jnp.take_along_axis(channels, orders.astype(jnp.int32), axis=1)
    return (flagged.reshape(-1).astype(jnp.int32), table.reshape(N_STN, N_CHAN, SLOTS).astype(jnp.int32))


def draw_flagged_ids(key, part):
    return plan_tables(key)[0]


def draw_work_plan(key, part):
    return plan_tables(key)[1]


def shard_levels(stream_key, shape, pieces, least, top_value):
    level = 1.0
    for position, shards_of in pieces:
        steps = jax.random.uniform(jax.random.fold_in(jax.random.fold_in(stream_key, 6), position), (shards_of,), jnp.float32, least / len(pieces), top_value / len(pieces))
        level = level * jnp.repeat(jnp.exp(steps), shape[position] // shards_of).reshape((-1,) + (1,) * (len(shape) - 1 - position))
    return level


def noise(rng, extent, deviation, bound, cuts=(), kind=jnp.bfloat16):
    gain = shard_levels(rng, extent, cuts, -0.22, 0.18) if cuts else 1.0
    values = jax.random.normal(rng, extent, jnp.float32) * deviation * gain
    return jnp.minimum(jnp.maximum(values, -bound), bound).astype(kind)


def setup_inputs(seed: int = 0) -> dict:
    keys = jax.random.split(jax.random.key(seed), 4)
    return {
        "voltages": noise(keys[0], (2, C, S, TIME), 1.0, 6.0, ((2, 32),)),
        "flagged_ids": draw_flagged_ids(jax.random.fold_in(keys[3], 71), 0),
        "work_plan": draw_work_plan(jax.random.fold_in(keys[3], 71), 0),
    }


def cross_power(block):
    station_count = block.shape[1]
    stacked = block.reshape(2 * station_count, block.shape[2])
    product = jnp.dot(stacked, stacked.T, preferred_element_type=jnp.float32)
    factor = 1.0 / block.shape[2]
    real_part = (product[:station_count, :station_count] + product[station_count:, station_count:]) * factor
    imag_part = (product[station_count:, :station_count] - product[:station_count, station_count:]) * factor
    visible = jnp.stack([real_part, imag_part]).astype(jnp.bfloat16)
    return visible, jnp.trace(real_part) / station_count


def reference(voltages, flagged_ids, work_plan):
    channel_ids = jnp.arange(C, dtype=jnp.int32)
    is_flagged = jnp.any(channel_ids[:, None] == flagged_ids[None, :], axis=1)

    def one_channel(channel):
        block = lax.dynamic_index_in_dim(voltages, channel, 1, keepdims=False)
        empty = (jnp.zeros((2, S, S), jnp.bfloat16), jnp.zeros((), jnp.float32))
        return lax.cond(is_flagged[channel], lambda: empty, lambda: cross_power(block))

    visibility, powers = lax.map(one_channel, channel_ids)
    return visibility, powers[work_plan]
```

```python
import functools

import jax
import jax.numpy as jnp
from jax import lax
from jax.experimental import pallas as pl
from jax.experimental.pallas import tpu as pltpu
from jax.sharding import PartitionSpec as P

MESH = pl.DeviceIdType.MESH
INNER = 2


def gather_kernel(n_stn, n_out, packed, own_out, power, full, made, recv1, send1, recv2, send2, send3, recv3, local3):
    stn = lax.axis_index("stn")
    chan = lax.axis_index("chan")
    outer, inner = chan // INNER, chan % INNER
    count, stations = packed.shape[1], packed.shape[2]
    scale = 1.0 / (packed.shape[3] // 2)
    has_left, has_right = outer > 0, outer < n_out - 1

    barrier = pltpu.get_barrier_semaphore()
    peers = []
    for step in range(1, n_stn * INNER):
        to_stn = lax.rem(stn + step // INNER, n_stn)
        to_inner = lax.rem(inner + step % INNER, INNER)
        peers.append((to_stn, to_inner))
        pl.semaphore_signal(barrier, inc=1, device_id=(to_stn, outer * INNER + to_inner), device_id_type=MESH)

    @pl.when(has_left)
    def _():
        pl.semaphore_signal(barrier, inc=1, device_id=(stn, chan - INNER), device_id_type=MESH)

    @pl.when(has_right)
    def _():
        pl.semaphore_signal(barrier, inc=1, device_id=(stn, chan + INNER), device_id_type=MESH)

    pl.semaphore_wait(barrier, len(peers) + jnp.where(has_left, 1, 0) + jnp.where(has_right, 1, 0))

    def turn(c):
        rows = pl.ds(pl.multiple_of(inner * stations, stations), stations)
        target = full.at[c, stn, outer, rows]
        for to_stn, to_inner in peers:
            pltpu.make_async_remote_copy(
                packed.at[to_stn * INNER + to_inner, c], target, send1.at[c], recv1.at[c],
                device_id=(to_stn, outer * INNER + to_inner), device_id_type=MESH,
            ).start()
        pltpu.make_async_copy(packed.at[stn * INNER + inner, c], target, recv1.at[c]).start()

    def line(c, block, way):
        part = full.at[c, :, block]
        return pltpu.make_async_remote_copy(
            part, part, send2.at[way, block, c], recv2.at[block, c],
            device_id=(stn, chan + (INNER if way else -INNER)), device_id_type=MESH,
        )

    def back(c):
        return pltpu.make_async_remote_copy(
            made.at[c, 1 - inner], own_out.at[inner * count + c], send3.at[c], recv3.at[c],
            device_id=(stn, outer * INNER + 1 - inner), device_id_type=MESH,
        )

    def keep(c):
        return pltpu.make_async_copy(made.at[c, inner], own_out.at[inner * count + c], local3.at[c])

    def correlate(c):
        span = 2 * stations
        pieces = n_out // INNER
        for half in range(INNER):
            left = full[c, outer, pl.ds(half * pieces, pieces)].reshape(pieces * span, -1)
            time = left.shape[1] // 2
            turned = jnp.concatenate([left[:, time:], -left[:, :time]], axis=1)
            both = jnp.concatenate([left, turned], axis=0)
            for col in range(n_stn):
                right = full[c, col].reshape(n_out * span, -1)
                product = lax.dot_general(both, right, (((1,), (1,)), ((), ())), preferred_element_type=jnp.float32)
                made[c, half, :, :, col * n_out * span:(col + 1) * n_out * span] = (
                    (product * scale).astype(jnp.bfloat16).reshape(2, pieces * span, n_out * span)
                )

    @pl.loop(0, count)
    def _(c):
        turn(c)

    @pl.loop(0, count + n_out - 1)
    def _(t):
        @pl.when(t < count)
        def _():
            part = full.at[t, :, outer]
            pltpu.make_async_copy(part, part, recv1.at[t]).wait()

            @pl.when(has_left)
            def _():
                line(t, outer, 0).start()

            @pl.when(has_right)
            def _():
                line(t, outer, 1).start()

        for d in range(1, n_out):
            c = t - d
            live = jnp.logical_and(c >= 0, c < count)

            @pl.when(jnp.logical_and(live, outer - d >= 0))
            def _():
                line(c, outer - d, 1).wait_recv()

                @pl.when(has_right)
                def _():
                    line(c, outer - d, 1).start()

            @pl.when(jnp.logical_and(live, outer + d < n_out))
            def _():
                line(c, outer + d, 0).wait_recv()

                @pl.when(has_left)
                def _():
                    line(c, outer + d, 0).start()

        done = t - (n_out - 1)

        @pl.when(done >= 0)
        def _():
            correlate(done)
            back(done).start()
            keep(done).start()

    for k in range(count // n_out):
        total = jnp.zeros((8, full.shape[4]), jnp.float32)
        for a in range(n_stn):
            values = full[outer * (count // n_out) + k, a].astype(jnp.float32)
            total = total + jnp.sum((values * values).reshape(-1, 8, full.shape[4]), axis=0)
        power[k] = jnp.full(power.shape[1:], jnp.sum(total))

    @pl.loop(0, count)
    def _(c):
        part = packed.at[pl.ds(0, n_stn * INNER - 1), c]
        pltpu.make_async_copy(part, part, send1.at[c]).wait()
        for block in range(n_out):
            @pl.when(jnp.logical_and(has_right, outer >= block))
            def _():
                line(c, block, 1).wait_send()

            @pl.when(jnp.logical_and(has_left, outer <= block))
            def _():
                line(c, block, 0).wait_send()

        back(c).wait_send()
        back(c).wait_recv()
        keep(c).wait()


def gather_and_correlate(packed, n_stn, n_out):
    dests, count, stations, depth = packed.shape
    total_rows = n_stn * n_out * INNER * stations
    rows = total_rows // (n_out * INNER)
    dma = pltpu.SemaphoreType.DMA
    return pl.pallas_call(
        functools.partial(gather_kernel, n_stn, n_out),
        out_shape=(
            jax.ShapeDtypeStruct((INNER * count, 2, rows, total_rows), jnp.bfloat16),
            jax.ShapeDtypeStruct((count // n_out, 8, 128), jnp.float32),
        ),
        in_specs=[pl.BlockSpec(memory_space=pltpu.VMEM)],
        out_specs=(pl.BlockSpec(memory_space=pl.ANY), pl.BlockSpec(memory_space=pltpu.VMEM)),
        scratch_shapes=[
            pltpu.VMEM((count, n_stn, n_out, INNER * stations, depth), jnp.bfloat16),
            pltpu.VMEM((count, INNER, 2, rows, total_rows), jnp.bfloat16),
            dma((count,)), dma((count,)),
            dma((n_out, count)), dma((2, n_out, count)),
            dma((count,)), dma((count,)), dma((count,)),
        ],
        compiler_params=pltpu.CompilerParams(
            collective_id=0, has_side_effects=True, vmem_limit_bytes=40 * 1024 * 1024
        ),
    )(packed)


def spread_kernel(table, live, rows, out):
    @pl.when(live[pl.program_id(0)] != 0)
    def _():
        out[...] = rows[...]

    @pl.when(live[pl.program_id(0)] == 0)
    def _():
        out[...] = jnp.zeros_like(out)


def spread(made, order, group_size):
    hit = order[None, :] == jnp.arange(group_size, dtype=jnp.int32)[:, None]
    table = jnp.sum(jnp.where(hit, jnp.arange(order.shape[0], dtype=jnp.int32)[None, :], 0), axis=1)
    live = jnp.any(hit, axis=1).astype(jnp.int32)
    block = (1,) + made.shape[1:]
    return pl.pallas_call(
        spread_kernel,
        out_shape=jax.ShapeDtypeStruct((group_size,) + made.shape[1:], made.dtype),
        grid_spec=pltpu.PrefetchScalarGridSpec(
            num_scalar_prefetch=2,
            grid=(group_size,),
            in_specs=[pl.BlockSpec(block, lambda c, table, live: (table[c], 0, 0, 0))],
            out_specs=pl.BlockSpec(block, lambda c, table, live: (c, 0, 0, 0)),
        ),
    )(table.astype(jnp.int32), live, made)


def correlate_gathered(packed, chan_idx, n_stn, n_out):
    dests, count, stations, depth = packed.shape
    n_chan = n_out * INNER
    shards = packed.reshape(n_stn, INNER * count, stations, depth)
    turned = lax.all_to_all(shards, "stn", split_axis=0, concat_axis=0, tiled=True)
    full = lax.all_gather(turned, "chan", axis=1)
    full = full.transpose(2, 0, 1, 3, 4).reshape(INNER * count, -1, depth)
    total_rows = full.shape[1]
    rows = total_rows // n_chan
    left = lax.dynamic_slice_in_dim(full, chan_idx * rows, rows, 1)
    time = depth // 2
    turned_left = jnp.concatenate([left[..., time:], -left[..., :time]], axis=-1)
    both = jnp.stack([left, turned_left], axis=1)
    made = jnp.einsum("cprk,csk->cprs", both, full, preferred_element_type=jnp.float32) * (1.0 / time)
    slots = count // n_out
    first = (chan_idx % INNER) * count + (chan_idx // INNER) * slots
    own = lax.dynamic_slice_in_dim(full, first, slots, 0).astype(jnp.float32)
    return made.astype(jnp.bfloat16), jnp.sum(own * own, axis=(1, 2))


def on_device(voltages, flagged_ids, work_plan):
    stn_idx, chan_idx = lax.axis_index("stn"), lax.axis_index("chan")
    n_stn, n_chan = lax.axis_size("stn"), lax.axis_size("chan")
    n_out = n_chan // INNER
    _, channels, stations, time = voltages.shape
    group_size = channels // n_stn
    slot_count = work_plan.shape[2]
    plan = work_plan.reshape(n_stn, n_out, INNER, slot_count).transpose(0, 2, 1, 3)
    count = n_out * slot_count
    packed = jnp.take(voltages, plan.reshape(-1), axis=1)
    packed = packed.transpose(1, 2, 0, 3).reshape(n_stn * INNER, count, stations, 2 * time)
    total_rows = stations * n_stn * n_chan
    if n_stn == n_out and stations % 16 == 0:
        made, power = gather_and_correlate(packed, n_stn, n_out)
        power = power[:, 0, 0]
    else:
        made, power = correlate_gathered(packed, chan_idx, n_stn, n_out)
    order = lax.dynamic_index_in_dim(plan, stn_idx, 0, keepdims=False).reshape(-1) - stn_idx * group_size
    visibility = spread(made, order, group_size)
    slot_power = (power * (1.0 / time) / total_rows).reshape(1, 1, slot_count)
    return visibility, slot_power


def solution(mesh):
    in_specs = (P(None, None, ("stn", "chan"), None), P(), P())
    out_specs = (P("stn", None, "chan", None), P("stn", "chan", None))
    return jax.shard_map(
        on_device, mesh=mesh, in_specs=in_specs, out_specs=out_specs, check_vma=False
    )
```

```python
import functools

import jax
import jax.numpy as jnp
from jax import lax
from jax.experimental import pallas as pl
from jax.experimental.pallas import tpu as pltpu
from jax.sharding import PartitionSpec as P

MESH = pl.DeviceIdType.MESH
AHEAD = 2
INNER = 2


def gather_kernel(n_stn, n_out, plan, voltages, own_out, power, packed, full, made, recv1, send1, recv2, send2, send3, recv3, local3):
    stn = lax.axis_index("stn")
    chan = lax.axis_index("chan")
    outer, inner = chan // INNER, chan % INNER
    count, stations = packed.shape[1], packed.shape[2]
    time = voltages.shape[3]
    scale = 1.0 / time
    has_left, has_right = outer > 0, outer < n_out - 1

    barrier = pltpu.get_barrier_semaphore()
    peers = []
    for step in range(1, n_stn * INNER):
        to_stn = lax.rem(stn + step // INNER, n_stn)
        to_inner = lax.rem(inner + step % INNER, INNER)
        peers.append((to_stn, to_inner))
        pl.semaphore_signal(barrier, inc=1, device_id=(to_stn, outer * INNER + to_inner), device_id_type=MESH)

    @pl.when(has_left)
    def _():
        pl.semaphore_signal(barrier, inc=1, device_id=(stn, chan - INNER), device_id_type=MESH)

    @pl.when(has_right)
    def _():
        pl.semaphore_signal(barrier, inc=1, device_id=(stn, chan + INNER), device_id_type=MESH)

    pl.semaphore_wait(barrier, len(peers) + jnp.where(has_left, 1, 0) + jnp.where(has_right, 1, 0))

    def turn(c):
        for dest in range(n_stn * INNER):
            channel = plan[dest * count + c]
            for part in range(2):
                packed[dest, c, :, part * time:(part + 1) * time] = voltages[part, channel]
        rows = pl.ds(pl.multiple_of(inner * stations, stations), stations)
        target = full.at[c, stn, outer, rows]
        for to_stn, to_inner in peers:
            pltpu.make_async_remote_copy(
                packed.at[to_stn * INNER + to_inner, c], target, send1.at[c], recv1.at[c],
                device_id=(to_stn, outer * INNER + to_inner), device_id_type=MESH,
            ).start()
        pltpu.make_async_copy(packed.at[stn * INNER + inner, c], target, recv1.at[c]).start()

    def line(c, block, way):
        part = full.at[c, :, block]
        return pltpu.make_async_remote_copy(
            part, part, send2.at[way, block, c], recv2.at[block, c],
            device_id=(stn, chan + (INNER if way else -INNER)), device_id_type=MESH,
        )

    def back(c):
        return pltpu.make_async_remote_copy(
            made.at[c, 1 - inner], own_out.at[inner * count + c], send3.at[c], recv3.at[c],
            device_id=(stn, outer * INNER + 1 - inner), device_id_type=MESH,
        )

    def keep(c):
        return pltpu.make_async_copy(made.at[c, inner], own_out.at[inner * count + c], local3.at[c])

    def correlate(c):
        span = 2 * stations
        pieces = n_out // INNER
        for half in range(INNER):
            left = full[c, outer, pl.ds(half * pieces, pieces)].reshape(pieces * span, -1)
            turned = jnp.concatenate([left[:, time:], -left[:, :time]], axis=1)
            both = jnp.concatenate([left, turned], axis=0)
            for col in range(n_stn):
                right = full[c, col].reshape(n_out * span, -1)
                product = lax.dot_general(both, right, (((1,), (1,)), ((), ())), preferred_element_type=jnp.float32)
                made[c, half, :, :, col * n_out * span:(col + 1) * n_out * span] = (
                    (product * scale).astype(jnp.bfloat16).reshape(2, pieces * span, n_out * span)
                )

    for c in range(AHEAD):
        turn(c)

    @pl.loop(0, count + n_out - 1)
    def _(t):
        @pl.when(t < count - AHEAD)
        def _():
            turn(t + AHEAD)

        @pl.when(t < count)
        def _():
            part = full.at[t, :, outer]
            pltpu.make_async_copy(part, part, recv1.at[t]).wait()

            @pl.when(has_left)
            def _():
                line(t, outer, 0).start()

            @pl.when(has_right)
            def _():
                line(t, outer, 1).start()

        for d in range(1, n_out):
            c = t - d
            live = jnp.logical_and(c >= 0, c < count)

            @pl.when(jnp.logical_and(live, outer - d >= 0))
            def _():
                line(c, outer - d, 1).wait_recv()

                @pl.when(has_right)
                def _():
                    line(c, outer - d, 1).start()

            @pl.when(jnp.logical_and(live, outer + d < n_out))
            def _():
                line(c, outer + d, 0).wait_recv()

                @pl.when(has_left)
                def _():
                    line(c, outer + d, 0).start()

        done = t - (n_out - 1)

        @pl.when(done >= 0)
        def _():
            correlate(done)
            back(done).start()
            keep(done).start()

    for k in range(count // n_out):
        total = jnp.zeros((8, full.shape[4]), jnp.float32)
        for a in range(n_stn):
            values = full[outer * (count // n_out) + k, a].astype(jnp.float32)
            total = total + jnp.sum((values * values).reshape(-1, 8, full.shape[4]), axis=0)
        power[0, 0, k] = jnp.sum(total) * scale / (n_stn * n_out * INNER * stations)

    @pl.loop(0, count)
    def _(c):
        part = packed.at[pl.ds(0, n_stn * INNER - 1), c]
        pltpu.make_async_copy(part, part, send1.at[c]).wait()
        for block in range(n_out):
            @pl.when(jnp.logical_and(has_right, outer >= block))
            def _():
                line(c, block, 1).wait_send()

            @pl.when(jnp.logical_and(has_left, outer <= block))
            def _():
                line(c, block, 0).wait_send()

        back(c).wait_send()
        back(c).wait_recv()
        keep(c).wait()


def gather_and_correlate(plan, voltages, n_stn, n_out):
    _, _, stations, time = voltages.shape
    count = plan.shape[0] // (n_stn * INNER)
    depth = 2 * time
    total_rows = n_stn * n_out * INNER * stations
    rows = total_rows // (n_out * INNER)
    dma = pltpu.SemaphoreType.DMA
    return pl.pallas_call(
        functools.partial(gather_kernel, n_stn, n_out),
        out_shape=(
            jax.ShapeDtypeStruct((INNER * count, 2, rows, total_rows), jnp.bfloat16),
            jax.ShapeDtypeStruct((1, 1, count // n_out), jnp.float32),
        ),
        in_specs=[pl.BlockSpec(memory_space=pltpu.SMEM), pl.BlockSpec(memory_space=pltpu.VMEM)],
        out_specs=(pl.BlockSpec(memory_space=pl.ANY), pl.BlockSpec(memory_space=pltpu.SMEM)),
        scratch_shapes=[
            pltpu.VMEM((n_stn * INNER, count, stations, depth), jnp.bfloat16),
            pltpu.VMEM((count, n_stn, n_out, INNER * stations, depth), jnp.bfloat16),
            pltpu.VMEM((count, INNER, 2, rows, total_rows), jnp.bfloat16),
            dma((count,)), dma((count,)),
            dma((n_out, count)), dma((2, n_out, count)),
            dma((count,)), dma((count,)), dma((count,)),
        ],
        compiler_params=pltpu.CompilerParams(
            collective_id=0, has_side_effects=True, vmem_limit_bytes=56 * 1024 * 1024
        ),
    )(plan, voltages)


def spread_kernel(plan, flagged, made, out, zeros, held, read_sem, write_sem, zero_sem):
    stn = lax.axis_index("stn")
    slots, group_size = made.shape[0], out.shape[0]
    first = stn * group_size
    idle = group_size - slots

    def read(j):
        return pltpu.make_async_copy(made.at[j], held.at[j], read_sem.at[j])

    def write(j):
        return pltpu.make_async_copy(held.at[j], out.at[plan[stn * slots + j] - first], write_sem.at[j])

    def clear(j):
        return pltpu.make_async_copy(zeros, out.at[flagged[stn * idle + j] - first], zero_sem.at[j])

    for j in range(slots):
        read(j).start()
    zeros[...] = jnp.zeros_like(zeros)
    for j in range(idle):
        clear(j).start()
    for j in range(slots):
        read(j).wait()
        write(j).start()
    for j in range(slots):
        write(j).wait()
    for j in range(idle):
        clear(j).wait()


def spread(plan, flagged, made, group_size):
    slots, idle = made.shape[0], group_size - made.shape[0]
    return pl.pallas_call(
        spread_kernel,
        out_shape=jax.ShapeDtypeStruct((group_size,) + made.shape[1:], made.dtype),
        in_specs=[pl.BlockSpec(memory_space=pltpu.SMEM)] * 2 + [pl.BlockSpec(memory_space=pl.ANY)],
        out_specs=pl.BlockSpec(memory_space=pl.ANY),
        scratch_shapes=[
            pltpu.VMEM(made.shape[1:], made.dtype),
            pltpu.VMEM(made.shape, made.dtype),
            pltpu.SemaphoreType.DMA((slots,)),
            pltpu.SemaphoreType.DMA((slots,)),
            pltpu.SemaphoreType.DMA((idle,)),
        ],
        compiler_params=pltpu.CompilerParams(vmem_limit_bytes=56 * 1024 * 1024),
    )(plan, flagged, made)


def correlate_gathered(plan, voltages, n_stn, n_out):
    _, _, stations, time = voltages.shape
    count, depth = plan.shape[0] // (n_stn * INNER), 2 * time
    chan_idx = lax.axis_index("chan")
    packed = jnp.take(voltages, plan, axis=1).transpose(1, 2, 0, 3)
    n_chan = n_out * INNER
    shards = packed.reshape(n_stn, INNER * count, stations, depth)
    turned = lax.all_to_all(shards, "stn", split_axis=0, concat_axis=0, tiled=True)
    full = lax.all_gather(turned, "chan", axis=1)
    full = full.transpose(2, 0, 1, 3, 4).reshape(INNER * count, -1, depth)
    total_rows = full.shape[1]
    rows = total_rows // n_chan
    left = lax.dynamic_slice_in_dim(full, chan_idx * rows, rows, 1)
    turned_left = jnp.concatenate([left[..., time:], -left[..., :time]], axis=-1)
    both = jnp.stack([left, turned_left], axis=1)
    made = jnp.einsum("cprk,csk->cprs", both, full, preferred_element_type=jnp.float32) * (1.0 / time)
    slots = count // n_out
    first = (chan_idx % INNER) * count + (chan_idx // INNER) * slots
    own = lax.dynamic_slice_in_dim(full, first, slots, 0).astype(jnp.float32)
    power = jnp.sum(own * own, axis=(1, 2)) * (1.0 / time) / total_rows
    return made.astype(jnp.bfloat16), power.reshape(1, 1, slots)


def on_device(voltages, flagged_ids, work_plan):
    n_stn, n_chan = lax.axis_size("stn"), lax.axis_size("chan")
    n_out = n_chan // INNER
    _, channels, stations, _ = voltages.shape
    slot_count = work_plan.shape[2]
    plan = work_plan.reshape(n_stn, n_out, INNER, slot_count).transpose(0, 2, 1, 3).reshape(-1)
    if n_stn == n_out and stations % 16 == 0:
        made, power = gather_and_correlate(plan, voltages, n_stn, n_out)
    else:
        made, power = correlate_gathered(plan, voltages, n_stn, n_out)
    return spread(plan, flagged_ids, made, channels // n_stn), power


def solution(mesh):
    in_specs = (P(None, None, ("stn", "chan"), None), P(), P())
    out_specs = (P("stn", None, "chan", None), P("stn", "chan", None))
    return jax.shard_map(
        on_device, mesh=mesh, in_specs=in_specs, out_specs=out_specs, check_vma=False
    )
```

```python
import functools

import jax
import jax.numpy as jnp
from jax import lax
from jax.experimental import pallas as pl
from jax.experimental.pallas import tpu as pltpu
from jax.sharding import PartitionSpec as P

MESH = pl.DeviceIdType.MESH
WINDOW = 2
LEAD = 1
AHEAD = 2
INNER = 2


def gather_kernel(n_stn, n_out, plan, voltages, own_out, power, packed, full, made, recv1, send1, recv2, send2, send3, recv3, local3):
    stn = lax.axis_index("stn")
    chan = lax.axis_index("chan")
    outer, inner = chan // INNER, chan % INNER
    count, stations = packed.shape[1], packed.shape[2]
    time = voltages.shape[3]
    scale = 1.0 / time
    has_left, has_right = outer > 0, outer < n_out - 1

    barrier = pltpu.get_barrier_semaphore()
    peers = []
    for step in range(1, n_stn * INNER):
        to_stn = lax.rem(stn + step // INNER, n_stn)
        to_inner = lax.rem(inner + step % INNER, INNER)
        peers.append((to_stn, to_inner))
        pl.semaphore_signal(barrier, inc=1, device_id=(to_stn, outer * INNER + to_inner), device_id_type=MESH)

    @pl.when(has_left)
    def _():
        pl.semaphore_signal(barrier, inc=1, device_id=(stn, chan - INNER), device_id_type=MESH)

    @pl.when(has_right)
    def _():
        pl.semaphore_signal(barrier, inc=1, device_id=(stn, chan + INNER), device_id_type=MESH)

    pl.semaphore_wait(barrier, len(peers) + jnp.where(has_left, 1, 0) + jnp.where(has_right, 1, 0))

    def turn(c):
        for dest in range(n_stn * INNER):
            channel = plan[dest * count + c]
            for part in range(2):
                packed[dest, c, :, part * time:(part + 1) * time] = voltages[part, channel]
        rows = pl.ds(pl.multiple_of(inner * stations, stations), stations)
        target = full.at[c, stn, outer, rows]
        for to_stn, to_inner in peers:
            pltpu.make_async_remote_copy(
                packed.at[to_stn * INNER + to_inner, c], target, send1.at[c], recv1.at[c],
                device_id=(to_stn, outer * INNER + to_inner), device_id_type=MESH,
            ).start()
        pltpu.make_async_copy(packed.at[stn * INNER + inner, c], target, recv1.at[c]).start()

    def line(c, block, way):
        part = full.at[c, :, block]
        return pltpu.make_async_remote_copy(
            part, part, send2.at[way, block, c], recv2.at[block, c],
            device_id=(stn, chan + (INNER if way else -INNER)), device_id_type=MESH,
        )

    def send(c, block, way):
        @pl.when(c >= WINDOW)
        def _():
            line(c - WINDOW, block, way).wait_send()

        line(c, block, way).start()

    def back(c):
        return pltpu.make_async_remote_copy(
            made.at[c, 1 - inner], own_out.at[inner * count + c], send3.at[c], recv3.at[c],
            device_id=(stn, outer * INNER + 1 - inner), device_id_type=MESH,
        )

    def keep(c):
        return pltpu.make_async_copy(made.at[c, inner], own_out.at[inner * count + c], local3.at[c])

    def correlate(c, half):
        span = INNER * stations
        pieces = n_out // INNER
        left = full[c, outer, pl.ds(half * pieces, pieces)].reshape(pieces * span, -1)
        turned = jnp.concatenate([left[:, time:], -left[:, :time]], axis=1)
        both = jnp.concatenate([left, turned], axis=0)
        for col in range(n_stn):
            right = full[c, col].reshape(n_out * span, -1)
            product = lax.dot_general(both, right, (((1,), (1,)), ((), ())), preferred_element_type=jnp.float32)
            made[c, half, :, :, col * n_out * span:(col + 1) * n_out * span] = (
                (product * scale).astype(jnp.bfloat16).reshape(2, pieces * span, n_out * span)
            )

    for c in range(AHEAD):
        turn(c)

    @pl.loop(0, count + LEAD)
    def _(t):
        @pl.when(t < count - AHEAD)
        def _():
            turn(t + AHEAD)

        @pl.when(t < count)
        def _():
            part = full.at[t, :, outer]
            pltpu.make_async_copy(part, part, recv1.at[t]).wait()

            @pl.when(has_left)
            def _():
                send(t, outer, 0)

            @pl.when(has_right)
            def _():
                send(t, outer, 1)

        c = t - LEAD
        live = c >= 0
        for d in range(1, n_out):

            @pl.when(jnp.logical_and(live, outer - d >= 0))
            def _():
                line(c, outer - d, 1).wait_recv()

                @pl.when(has_right)
                def _():
                    send(c, outer - d, 1)

            @pl.when(jnp.logical_and(live, outer + d < n_out))
            def _():
                line(c, outer + d, 0).wait_recv()

                @pl.when(has_left)
                def _():
                    send(c, outer + d, 0)

        @pl.when(live)
        def _():
            correlate(c, 1 - inner)
            back(c).start()
            correlate(c, inner)
            keep(c).start()

    for k in range(count // n_out):
        total = jnp.zeros((8, full.shape[4]), jnp.float32)
        for a in range(n_stn):
            values = full[outer * (count // n_out) + k, a].astype(jnp.float32)
            total = total + jnp.sum((values * values).reshape(-1, 8, full.shape[4]), axis=0)
        power[0, 0, k] = jnp.sum(total) * scale / (n_stn * n_out * INNER * stations)

    @pl.loop(0, count)
    def _(c):
        part = packed.at[pl.ds(0, n_stn * INNER - 1), c]
        pltpu.make_async_copy(part, part, send1.at[c]).wait()

        @pl.when(c >= count - WINDOW)
        def _():
            for block in range(n_out):
                @pl.when(jnp.logical_and(has_right, outer >= block))
                def _():
                    line(c, block, 1).wait_send()

                @pl.when(jnp.logical_and(has_left, outer <= block))
                def _():
                    line(c, block, 0).wait_send()

        back(c).wait_send()
        back(c).wait_recv()
        keep(c).wait()


def gather_and_correlate(plan, voltages, n_stn, n_out):
    _, _, stations, time = voltages.shape
    count = plan.shape[0] // (n_stn * INNER)
    depth = 2 * time
    total_rows = n_stn * n_out * INNER * stations
    rows = total_rows // (n_out * INNER)
    dma = pltpu.SemaphoreType.DMA
    return pl.pallas_call(
        functools.partial(gather_kernel, n_stn, n_out),
        out_shape=(
            jax.ShapeDtypeStruct((INNER * count, 2, rows, total_rows), jnp.bfloat16),
            jax.ShapeDtypeStruct((1, 1, count // n_out), jnp.float32),
        ),
        in_specs=[pl.BlockSpec(memory_space=pltpu.SMEM), pl.BlockSpec(memory_space=pltpu.VMEM)],
        out_specs=(pl.BlockSpec(memory_space=pl.ANY), pl.BlockSpec(memory_space=pltpu.SMEM)),
        scratch_shapes=[
            pltpu.VMEM((n_stn * INNER, count, stations, depth), jnp.bfloat16),
            pltpu.VMEM((count, n_stn, n_out, INNER * stations, depth), jnp.bfloat16),
            pltpu.VMEM((count, INNER, 2, rows, total_rows), jnp.bfloat16),
            dma((count,)), dma((count,)),
            dma((n_out, count)), dma((2, n_out, count)),
            dma((count,)), dma((count,)), dma((count,)),
        ],
        compiler_params=pltpu.CompilerParams(
            collective_id=0, has_side_effects=True, vmem_limit_bytes=56 * 1024 * 1024
        ),
    )(plan, voltages)


def spread_kernel(plan, flagged, made, out, zeros, held, read_sem, write_sem, zero_sem):
    stn = lax.axis_index("stn")
    slots, group_size = made.shape[0], out.shape[0]
    first = stn * group_size
    idle = group_size - slots

    def read(j):
        return pltpu.make_async_copy(made.at[j], held.at[j], read_sem.at[j])

    def write(j):
        return pltpu.make_async_copy(held.at[j], out.at[plan[stn * slots + j] - first], write_sem.at[j])

    def clear(j):
        return pltpu.make_async_copy(zeros, out.at[flagged[stn * idle + j] - first], zero_sem.at[j])

    for j in range(slots):
        read(j).start()
    zeros[...] = jnp.zeros_like(zeros)
    for j in range(idle):
        clear(j).start()
    for j in range(slots):
        read(j).wait()
        write(j).start()
    for j in range(slots):
        write(j).wait()
    for j in range(idle):
        clear(j).wait()


def spread(plan, flagged, made, group_size):
    slots, idle = made.shape[0], group_size - made.shape[0]
    return pl.pallas_call(
        spread_kernel,
        out_shape=jax.ShapeDtypeStruct((group_size,) + made.shape[1:], made.dtype),
        in_specs=[pl.BlockSpec(memory_space=pltpu.SMEM)] * 2 + [pl.BlockSpec(memory_space=pl.ANY)],
        out_specs=pl.BlockSpec(memory_space=pl.ANY),
        scratch_shapes=[
            pltpu.VMEM(made.shape[1:], made.dtype),
            pltpu.VMEM(made.shape, made.dtype),
            pltpu.SemaphoreType.DMA((slots,)),
            pltpu.SemaphoreType.DMA((slots,)),
            pltpu.SemaphoreType.DMA((idle,)),
        ],
        compiler_params=pltpu.CompilerParams(vmem_limit_bytes=56 * 1024 * 1024),
    )(plan, flagged, made)


def correlate_gathered(plan, voltages, n_stn, n_out):
    _, _, stations, time = voltages.shape
    count, depth = plan.shape[0] // (n_stn * INNER), 2 * time
    chan_idx = lax.axis_index("chan")
    packed = jnp.take(voltages, plan, axis=1).transpose(1, 2, 0, 3)
    n_chan = n_out * INNER
    shards = packed.reshape(n_stn, INNER * count, stations, depth)
    turned = lax.all_to_all(shards, "stn", split_axis=0, concat_axis=0, tiled=True)
    full = lax.all_gather(turned, "chan", axis=1)
    full = full.transpose(2, 0, 1, 3, 4).reshape(INNER * count, -1, depth)
    total_rows = full.shape[1]
    rows = total_rows // n_chan
    left = lax.dynamic_slice_in_dim(full, chan_idx * rows, rows, 1)
    turned_left = jnp.concatenate([left[..., time:], -left[..., :time]], axis=-1)
    both = jnp.stack([left, turned_left], axis=1)
    made = jnp.einsum("cprk,csk->cprs", both, full, preferred_element_type=jnp.float32) * (1.0 / time)
    slots = count // n_out
    first = (chan_idx % INNER) * count + (chan_idx // INNER) * slots
    own = lax.dynamic_slice_in_dim(full, first, slots, 0).astype(jnp.float32)
    power = jnp.sum(own * own, axis=(1, 2)) * (1.0 / time) / total_rows
    return made.astype(jnp.bfloat16), power.reshape(1, 1, slots)


def on_device(voltages, flagged_ids, work_plan):
    n_stn, n_chan = lax.axis_size("stn"), lax.axis_size("chan")
    n_out = n_chan // INNER
    _, channels, stations, _ = voltages.shape
    slot_count = work_plan.shape[2]
    plan = work_plan.reshape(n_stn, n_out, INNER, slot_count).transpose(0, 2, 1, 3).reshape(-1)
    if n_stn == n_out and stations % 16 == 0:
        made, power = gather_and_correlate(plan, voltages, n_stn, n_out)
    else:
        made, power = correlate_gathered(plan, voltages, n_stn, n_out)
    return spread(plan, flagged_ids, made, channels // n_stn), power


def solution(mesh):
    in_specs = (P(None, None, ("stn", "chan"), None), P(), P())
    out_specs = (P("stn", None, "chan", None), P("stn", "chan", None))
    return jax.shard_map(
        on_device, mesh=mesh, in_specs=in_specs, out_specs=out_specs, check_vma=False
    )
```

```python
import functools

import jax
import jax.numpy as jnp
from jax import lax
from jax.experimental import pallas as pl
from jax.experimental.pallas import tpu as pltpu
from jax.sharding import PartitionSpec as P

MESH = pl.DeviceIdType.MESH
WINDOW = 2
LEAD = 1
AHEAD = 2
INNER = 2


def gather_kernel(n_stn, n_out, plan, voltages, own_out, power, packed, full, made, recv1, send1, recv2, send2, send3, recv3, local3):
    stn = lax.axis_index("stn")
    chan = lax.axis_index("chan")
    outer, inner = chan // INNER, chan % INNER
    count, stations = packed.shape[1], packed.shape[2]
    time = voltages.shape[3]
    scale = 1.0 / time
    has_left, has_right = outer > 0, outer < n_out - 1

    barrier = pltpu.get_barrier_semaphore()
    peers = []
    for step in range(1, n_stn * INNER):
        to_stn = lax.rem(stn + step // INNER, n_stn)
        to_inner = lax.rem(inner + step % INNER, INNER)
        peers.append((to_stn, to_inner))
        pl.semaphore_signal(barrier, inc=1, device_id=(to_stn, outer * INNER + to_inner), device_id_type=MESH)

    @pl.when(has_left)
    def _():
        pl.semaphore_signal(barrier, inc=1, device_id=(stn, chan - INNER), device_id_type=MESH)

    @pl.when(has_right)
    def _():
        pl.semaphore_signal(barrier, inc=1, device_id=(stn, chan + INNER), device_id_type=MESH)

    pl.semaphore_wait(barrier, len(peers) + jnp.where(has_left, 1, 0) + jnp.where(has_right, 1, 0))

    def turn(c):
        for dest in range(n_stn * INNER):
            channel = plan[dest * count + c]
            for part in range(2):
                packed[dest, c, :, part * time:(part + 1) * time] = voltages[part, channel]
        rows = pl.ds(pl.multiple_of(inner * stations, stations), stations)
        target = full.at[c, stn, outer, rows]
        for to_stn, to_inner in peers:
            pltpu.make_async_remote_copy(
                packed.at[to_stn * INNER + to_inner, c], target, send1.at[c], recv1.at[c],
                device_id=(to_stn, outer * INNER + to_inner), device_id_type=MESH,
            ).start()
        pltpu.make_async_copy(packed.at[stn * INNER + inner, c], target, recv1.at[c]).start()

    def line(c, block, way):
        part = full.at[c, :, block]
        return pltpu.make_async_remote_copy(
            part, part, send2.at[way, block, c], recv2.at[block, c],
            device_id=(stn, chan + (INNER if way else -INNER)), device_id_type=MESH,
        )

    def send(c, block, way):
        @pl.when(c >= WINDOW)
        def _():
            line(c - WINDOW, block, way).wait_send()

        line(c, block, way).start()

    def back(c):
        return pltpu.make_async_remote_copy(
            made.at[c, 1 - inner], own_out.at[inner * count + c], send3.at[c], recv3.at[c],
            device_id=(stn, outer * INNER + 1 - inner), device_id_type=MESH,
        )

    def keep(c):
        return pltpu.make_async_copy(made.at[c, inner], own_out.at[inner * count + c], local3.at[c])

    def correlate(c, half):
        span = INNER * stations
        pieces = n_out // INNER
        left = full[c, outer, pl.ds(half * pieces, pieces)].reshape(pieces * span, -1)
        turned = jnp.concatenate([left[:, time:], -left[:, :time]], axis=1)
        both = jnp.concatenate([left, turned], axis=0)
        for col in range(n_stn):
            right = full[c, col].reshape(n_out * span, -1)
            product = lax.dot_general(both, right, (((1,), (1,)), ((), ())), preferred_element_type=jnp.float32)
            made[c, half, :, :, col * n_out * span:(col + 1) * n_out * span] = (
                (product * scale).astype(jnp.bfloat16).reshape(2, pieces * span, n_out * span)
            )

    for c in range(AHEAD):
        turn(c)

    @pl.loop(0, count + LEAD)
    def _(t):
        @pl.when(t < count - AHEAD)
        def _():
            turn(t + AHEAD)

        @pl.when(t < count)
        def _():
            part = full.at[t, :, outer]
            pltpu.make_async_copy(part, part, recv1.at[t]).wait()

            @pl.when(has_left)
            def _():
                send(t, outer, 0)

            @pl.when(has_right)
            def _():
                send(t, outer, 1)

        c = t - LEAD
        live = c >= 0
        for d in range(1, n_out):

            @pl.when(jnp.logical_and(live, outer - d >= 0))
            def _():
                line(c, outer - d, 1).wait_recv()

                @pl.when(has_right)
                def _():
                    send(c, outer - d, 1)

            @pl.when(jnp.logical_and(live, outer + d < n_out))
            def _():
                line(c, outer + d, 0).wait_recv()

                @pl.when(has_left)
                def _():
                    send(c, outer + d, 0)

        @pl.when(live)
        def _():
            correlate(c, 1 - inner)
            back(c).start()
            correlate(c, inner)
            keep(c).start()

    for k in range(count // n_out):
        total = jnp.zeros((8, full.shape[4]), jnp.float32)
        for a in range(n_stn):
            values = full[outer * (count // n_out) + k, a].astype(jnp.float32)
            total = total + jnp.sum((values * values).reshape(-1, 8, full.shape[4]), axis=0)
        power[0, 0, k] = jnp.sum(total) * scale / (n_stn * n_out * INNER * stations)

    @pl.loop(0, count)
    def _(c):
        part = packed.at[pl.ds(0, n_stn * INNER - 1), c]
        pltpu.make_async_copy(part, part, send1.at[c]).wait()

        @pl.when(c >= count - WINDOW)
        def _():
            for block in range(n_out):
                @pl.when(jnp.logical_and(has_right, outer >= block))
                def _():
                    line(c, block, 1).wait_send()

                @pl.when(jnp.logical_and(has_left, outer <= block))
                def _():
                    line(c, block, 0).wait_send()

        back(c).wait_send()
        back(c).wait_recv()
        keep(c).wait()


def gather_and_correlate(plan, voltages, n_stn, n_out):
    _, _, stations, time = voltages.shape
    count = plan.shape[0] // (n_stn * INNER)
    depth = 2 * time
    total_rows = n_stn * n_out * INNER * stations
    rows = total_rows // (n_out * INNER)
    dma = pltpu.SemaphoreType.DMA
    return pl.pallas_call(
        functools.partial(gather_kernel, n_stn, n_out),
        out_shape=(
            pltpu.VMEM((INNER * count, 2, rows, total_rows), jnp.bfloat16),
            jax.ShapeDtypeStruct((1, 1, count // n_out), jnp.float32),
        ),
        in_specs=[pl.BlockSpec(memory_space=pltpu.SMEM), pl.BlockSpec(memory_space=pltpu.VMEM)],
        out_specs=(pl.BlockSpec(memory_space=pl.ANY), pl.BlockSpec(memory_space=pltpu.SMEM)),
        scratch_shapes=[
            pltpu.VMEM((n_stn * INNER, count, stations, depth), jnp.bfloat16),
            pltpu.VMEM((count, n_stn, n_out, INNER * stations, depth), jnp.bfloat16),
            pltpu.VMEM((count, INNER, 2, rows, total_rows), jnp.bfloat16),
            dma((count,)), dma((count,)),
            dma((n_out, count)), dma((2, n_out, count)),
            dma((count,)), dma((count,)), dma((count,)),
        ],
        compiler_params=pltpu.CompilerParams(
            collective_id=0, has_side_effects=True, vmem_limit_bytes=30 * 1024 * 1024
        ),
    )(plan, voltages)


def spread_kernel(plan, flagged, made, out, zeros, write_sem, zero_sem):
    stn = lax.axis_index("stn")
    slots, group_size = made.shape[0], out.shape[0]
    first = stn * group_size
    idle = group_size - slots

    def write(j):
        return pltpu.make_async_copy(made.at[j], out.at[plan[stn * slots + j] - first], write_sem.at[j])

    def clear(j):
        return pltpu.make_async_copy(zeros, out.at[flagged[stn * idle + j] - first], zero_sem.at[j])

    for j in range(slots):
        write(j).start()
    zeros[...] = jnp.zeros_like(zeros)
    for j in range(idle):
        clear(j).start()
    for j in range(slots):
        write(j).wait()
    for j in range(idle):
        clear(j).wait()


def spread(plan, flagged, made, group_size):
    slots, idle = made.shape[0], group_size - made.shape[0]
    return pl.pallas_call(
        spread_kernel,
        out_shape=jax.ShapeDtypeStruct((group_size,) + made.shape[1:], made.dtype),
        in_specs=[pl.BlockSpec(memory_space=pltpu.SMEM)] * 2 + [pl.BlockSpec(memory_space=pl.ANY)],
        out_specs=pl.BlockSpec(memory_space=pl.ANY),
        scratch_shapes=[
            pltpu.VMEM(made.shape[1:], made.dtype),
            pltpu.SemaphoreType.DMA((slots,)),
            pltpu.SemaphoreType.DMA((idle,)),
        ],
        compiler_params=pltpu.CompilerParams(vmem_limit_bytes=16 * 1024 * 1024),
    )(plan, flagged, made)


def correlate_gathered(plan, voltages, n_stn, n_out):
    _, _, stations, time = voltages.shape
    count, depth = plan.shape[0] // (n_stn * INNER), 2 * time
    chan_idx = lax.axis_index("chan")
    packed = jnp.take(voltages, plan, axis=1).transpose(1, 2, 0, 3)
    n_chan = n_out * INNER
    shards = packed.reshape(n_stn, INNER * count, stations, depth)
    turned = lax.all_to_all(shards, "stn", split_axis=0, concat_axis=0, tiled=True)
    full = lax.all_gather(turned, "chan", axis=1)
    full = full.transpose(2, 0, 1, 3, 4).reshape(INNER * count, -1, depth)
    total_rows = full.shape[1]
    rows = total_rows // n_chan
    left = lax.dynamic_slice_in_dim(full, chan_idx * rows, rows, 1)
    turned_left = jnp.concatenate([left[..., time:], -left[..., :time]], axis=-1)
    both = jnp.stack([left, turned_left], axis=1)
    made = jnp.einsum("cprk,csk->cprs", both, full, preferred_element_type=jnp.float32) * (1.0 / time)
    slots = count // n_out
    first = (chan_idx % INNER) * count + (chan_idx // INNER) * slots
    own = lax.dynamic_slice_in_dim(full, first, slots, 0).astype(jnp.float32)
    power = jnp.sum(own * own, axis=(1, 2)) * (1.0 / time) / total_rows
    return made.astype(jnp.bfloat16), power.reshape(1, 1, slots)


def on_device(voltages, flagged_ids, work_plan):
    n_stn, n_chan = lax.axis_size("stn"), lax.axis_size("chan")
    n_out = n_chan // INNER
    _, channels, stations, _ = voltages.shape
    slot_count = work_plan.shape[2]
    plan = work_plan.reshape(n_stn, n_out, INNER, slot_count).transpose(0, 2, 1, 3).reshape(-1)
    if n_stn == n_out and stations % 16 == 0:
        made, power = gather_and_correlate(plan, voltages, n_stn, n_out)
    else:
        made, power = correlate_gathered(plan, voltages, n_stn, n_out)
    return spread(plan, flagged_ids, made, channels // n_stn), power


def solution(mesh):
    in_specs = (P(None, None, ("stn", "chan"), None), P(), P())
    out_specs = (P("stn", None, "chan", None), P("stn", "chan", None))
    return jax.shard_map(
        on_device, mesh=mesh, in_specs=in_specs, out_specs=out_specs, check_vma=False
    )
```

```python
import functools

import jax
import jax.numpy as jnp
from jax import lax
from jax.experimental import pallas as pl
from jax.experimental.pallas import tpu as pltpu
from jax.sharding import PartitionSpec as P

MESH = pl.DeviceIdType.MESH
WINDOW = 2
LEAD = 1
AHEAD = 2
INNER = 2


def gather_kernel(n_stn, n_out, plan, voltages, own_out, power, packed, full, extra, made, recv1, send1, recv2, send2, send3, recv3, local3, send4, recv4):
    stn = lax.axis_index("stn")
    chan = lax.axis_index("chan")
    outer, inner = chan // INNER, chan % INNER
    count, stations = packed.shape[1], packed.shape[2]
    time = voltages.shape[3]
    scale = 1.0 / time
    last = count - 1
    has_left, has_right = outer > 0, outer < n_out - 1

    barrier = pltpu.get_barrier_semaphore()
    peers = []
    for step in range(1, n_stn * INNER):
        to_stn = lax.rem(stn + step // INNER, n_stn)
        to_inner = lax.rem(inner + step % INNER, INNER)
        peers.append((to_stn, to_inner))
        pl.semaphore_signal(barrier, inc=1, device_id=(to_stn, outer * INNER + to_inner), device_id_type=MESH)

    @pl.when(has_left)
    def _():
        pl.semaphore_signal(barrier, inc=1, device_id=(stn, chan - INNER), device_id_type=MESH)

    @pl.when(has_right)
    def _():
        pl.semaphore_signal(barrier, inc=1, device_id=(stn, chan + INNER), device_id_type=MESH)

    pl.semaphore_wait(barrier, len(peers) + jnp.where(has_left, 1, 0) + jnp.where(has_right, 1, 0))

    def turn(c):
        for dest in range(n_stn * INNER):
            channel = plan[dest * count + c]
            for part in range(2):
                packed[dest, c, :, part * time:(part + 1) * time] = voltages[part, channel]
        rows = pl.ds(pl.multiple_of(inner * stations, stations), stations)
        target = full.at[c, stn, outer, rows]
        for to_stn, to_inner in peers:
            pltpu.make_async_remote_copy(
                packed.at[to_stn * INNER + to_inner, c], target, send1.at[c], recv1.at[c],
                device_id=(to_stn, outer * INNER + to_inner), device_id_type=MESH,
            ).start()
        pltpu.make_async_copy(packed.at[stn * INNER + inner, c], target, recv1.at[c]).start()

    def line(c, block, way):
        part = full.at[c, :, block]
        return pltpu.make_async_remote_copy(
            part, part, send2.at[way, block, c], recv2.at[block, c],
            device_id=(stn, chan + (INNER if way else -INNER)), device_id_type=MESH,
        )

    def send(c, block, way):
        @pl.when(c >= WINDOW)
        def _():
            line(c - WINDOW, block, way).wait_send()

        line(c, block, way).start()

    def back(c):
        return pltpu.make_async_remote_copy(
            made.at[c, 1 - inner], own_out.at[inner * count + c], send3.at[c], recv3.at[c],
            device_id=(stn, outer * INNER + 1 - inner), device_id_type=MESH,
        )

    def keep(c, half, sem):
        return pltpu.make_async_copy(made.at[c, half], own_out.at[half * count + c], local3.at[sem])

    def share(block):
        return pltpu.make_async_remote_copy(
            full.at[last, :, block], extra.at[:, block], send4.at[block], recv4.at[block],
            device_id=(stn, outer * INNER + 1 - inner), device_id_type=MESH,
        )

    def correlate(source, c, rows_of, half):
        span = INNER * stations
        pieces = n_out // INNER
        left = source[outer, pl.ds(rows_of * pieces, pieces)].reshape(pieces * span, -1)
        turned = jnp.concatenate([left[:, time:], -left[:, :time]], axis=1)
        both = jnp.concatenate([left, turned], axis=0)
        for col in range(n_stn):
            right = source[col].reshape(n_out * span, -1)
            product = lax.dot_general(both, right, (((1,), (1,)), ((), ())), preferred_element_type=jnp.float32)
            made[c, half, :, :, col * n_out * span:(col + 1) * n_out * span] = (
                (product * scale).astype(jnp.bfloat16).reshape(2, pieces * span, n_out * span)
            )

    for c in range(AHEAD):
        turn(c)

    @pl.loop(0, count + LEAD)
    def _(t):
        @pl.when(t < count - AHEAD)
        def _():
            turn(t + AHEAD)

        @pl.when(t < count)
        def _():
            part = full.at[t, :, outer]
            pltpu.make_async_copy(part, part, recv1.at[t]).wait()

            @pl.when(has_left)
            def _():
                send(t, outer, 0)

            @pl.when(has_right)
            def _():
                send(t, outer, 1)

            @pl.when(t == last)
            def _():
                share(outer).start()

        c = t - LEAD
        live = c >= 0
        for d in range(1, n_out):

            @pl.when(jnp.logical_and(live, outer - d >= 0))
            def _():
                line(c, outer - d, 1).wait_recv()

                @pl.when(has_right)
                def _():
                    send(c, outer - d, 1)

                @pl.when(c == last)
                def _():
                    share(outer - d).start()

            @pl.when(jnp.logical_and(live, outer + d < n_out))
            def _():
                line(c, outer + d, 0).wait_recv()

                @pl.when(has_left)
                def _():
                    send(c, outer + d, 0)

                @pl.when(c == last)
                def _():
                    share(outer + d).start()

        @pl.when(live)
        def _():
            @pl.when(c < last)
            def _():
                correlate(full.at[c], c, 1 - inner, 1 - inner)
                back(c).start()

            correlate(full.at[c], c, inner, inner)
            keep(c, inner, c).start()

    for k in range(count // n_out):
        total = jnp.zeros((8, full.shape[4]), jnp.float32)
        for a in range(n_stn):
            values = full[outer * (count // n_out) + k, a].astype(jnp.float32)
            total = total + jnp.sum((values * values).reshape(-1, 8, full.shape[4]), axis=0)
        power[0, 0, k] = jnp.sum(total) * scale / (n_stn * n_out * INNER * stations)

    for block in range(n_out):
        share(block).wait_recv()
    correlate(extra, last, inner, 1 - inner)
    keep(last, 1 - inner, count).start()

    @pl.loop(0, count)
    def _(c):
        part = packed.at[pl.ds(0, n_stn * INNER - 1), c]
        pltpu.make_async_copy(part, part, send1.at[c]).wait()

        @pl.when(c >= count - WINDOW)
        def _():
            for block in range(n_out):
                @pl.when(jnp.logical_and(has_right, outer >= block))
                def _():
                    line(c, block, 1).wait_send()

                @pl.when(jnp.logical_and(has_left, outer <= block))
                def _():
                    line(c, block, 0).wait_send()

        @pl.when(c < last)
        def _():
            back(c).wait_send()
            back(c).wait_recv()

        keep(c, inner, c).wait()

    keep(last, 1 - inner, count).wait()
    for block in range(n_out):
        share(block).wait_send()


def gather_and_correlate(plan, voltages, n_stn, n_out):
    _, _, stations, time = voltages.shape
    count = plan.shape[0] // (n_stn * INNER)
    depth = 2 * time
    total_rows = n_stn * n_out * INNER * stations
    rows = total_rows // (n_out * INNER)
    dma = pltpu.SemaphoreType.DMA
    return pl.pallas_call(
        functools.partial(gather_kernel, n_stn, n_out),
        out_shape=(
            pltpu.VMEM((INNER * count, 2, rows, total_rows), jnp.bfloat16),
            jax.ShapeDtypeStruct((1, 1, count // n_out), jnp.float32),
        ),
        in_specs=[pl.BlockSpec(memory_space=pltpu.SMEM), pl.BlockSpec(memory_space=pltpu.VMEM)],
        out_specs=(pl.BlockSpec(memory_space=pl.ANY), pl.BlockSpec(memory_space=pltpu.SMEM)),
        scratch_shapes=[
            pltpu.VMEM((n_stn * INNER, count, stations, depth), jnp.bfloat16),
            pltpu.VMEM((count, n_stn, n_out, INNER * stations, depth), jnp.bfloat16),
            pltpu.VMEM((n_stn, n_out, INNER * stations, depth), jnp.bfloat16),
            pltpu.VMEM((count, INNER, 2, rows, total_rows), jnp.bfloat16),
            dma((count,)), dma((count,)),
            dma((n_out, count)), dma((2, n_out, count)),
            dma((count,)), dma((count,)), dma((count + 1,)),
            dma((n_out,)), dma((n_out,)),
        ],
        compiler_params=pltpu.CompilerParams(
            collective_id=0, has_side_effects=True, vmem_limit_bytes=30 * 1024 * 1024
        ),
    )(plan, voltages)


def spread_kernel(plan, flagged, made, out, zeros, write_sem, zero_sem):
    stn = lax.axis_index("stn")
    slots, group_size = made.shape[0], out.shape[0]
    first = stn * group_size
    idle = group_size - slots

    def write(j):
        return pltpu.make_async_copy(made.at[j], out.at[plan[stn * slots + j] - first], write_sem.at[j])

    def clear(j):
        return pltpu.make_async_copy(zeros, out.at[flagged[stn * idle + j] - first], zero_sem.at[j])

    for j in range(slots):
        write(j).start()
    zeros[...] = jnp.zeros_like(zeros)
    for j in range(idle):
        clear(j).start()
    for j in range(slots):
        write(j).wait()
    for j in range(idle):
        clear(j).wait()


def spread(plan, flagged, made, group_size):
    slots, idle = made.shape[0], group_size - made.shape[0]
    return pl.pallas_call(
        spread_kernel,
        out_shape=jax.ShapeDtypeStruct((group_size,) + made.shape[1:], made.dtype),
        in_specs=[pl.BlockSpec(memory_space=pltpu.SMEM)] * 2 + [pl.BlockSpec(memory_space=pl.ANY)],
        out_specs=pl.BlockSpec(memory_space=pl.ANY),
        scratch_shapes=[
            pltpu.VMEM(made.shape[1:], made.dtype),
            pltpu.SemaphoreType.DMA((slots,)),
            pltpu.SemaphoreType.DMA((idle,)),
        ],
        compiler_params=pltpu.CompilerParams(vmem_limit_bytes=16 * 1024 * 1024),
    )(plan, flagged, made)


def correlate_gathered(plan, voltages, n_stn, n_out):
    _, _, stations, time = voltages.shape
    count, depth = plan.shape[0] // (n_stn * INNER), 2 * time
    chan_idx = lax.axis_index("chan")
    packed = jnp.take(voltages, plan, axis=1).transpose(1, 2, 0, 3)
    n_chan = n_out * INNER
    shards = packed.reshape(n_stn, INNER * count, stations, depth)
    turned = lax.all_to_all(shards, "stn", split_axis=0, concat_axis=0, tiled=True)
    full = lax.all_gather(turned, "chan", axis=1)
    full = full.transpose(2, 0, 1, 3, 4).reshape(INNER * count, -1, depth)
    total_rows = full.shape[1]
    rows = total_rows // n_chan
    left = lax.dynamic_slice_in_dim(full, chan_idx * rows, rows, 1)
    turned_left = jnp.concatenate([left[..., time:], -left[..., :time]], axis=-1)
    both = jnp.stack([left, turned_left], axis=1)
    made = jnp.einsum("cprk,csk->cprs", both, full, preferred_element_type=jnp.float32) * (1.0 / time)
    slots = count // n_out
    first = (chan_idx % INNER) * count + (chan_idx // INNER) * slots
    own = lax.dynamic_slice_in_dim(full, first, slots, 0).astype(jnp.float32)
    power = jnp.sum(own * own, axis=(1, 2)) * (1.0 / time) / total_rows
    return made.astype(jnp.bfloat16), power.reshape(1, 1, slots)


def on_device(voltages, flagged_ids, work_plan):
    n_stn, n_chan = lax.axis_size("stn"), lax.axis_size("chan")
    n_out = n_chan // INNER
    _, channels, stations, _ = voltages.shape
    slot_count = work_plan.shape[2]
    plan = work_plan.reshape(n_stn, n_out, INNER, slot_count).transpose(0, 2, 1, 3).reshape(-1)
    if n_stn == n_out and stations % 16 == 0:
        made, power = gather_and_correlate(plan, voltages, n_stn, n_out)
    else:
        made, power = correlate_gathered(plan, voltages, n_stn, n_out)
    return spread(plan, flagged_ids, made, channels // n_stn), power


def solution(mesh):
    in_specs = (P(None, None, ("stn", "chan"), None), P(), P())
    out_specs = (P("stn", None, "chan", None), P("stn", "chan", None))
    return jax.shard_map(
        on_device, mesh=mesh, in_specs=in_specs, out_specs=out_specs, check_vma=False
    )
```

```python
import functools

import jax
import jax.numpy as jnp
from jax import lax
from jax.experimental import pallas as pl
from jax.experimental.pallas import tpu as pltpu
from jax.sharding import PartitionSpec as P

MESH = pl.DeviceIdType.MESH
WINDOW = 2
LEAD = 1
AHEAD = 2
INNER = 2


def gather_kernel(n_stn, n_out, plan, voltages, own_out, power, packed, full, made, recv1, send1, recv2, send2, send3, recv3, local3):
    stn = lax.axis_index("stn")
    chan = lax.axis_index("chan")
    outer, inner = chan // INNER, chan % INNER
    count, stations = packed.shape[1], packed.shape[2]
    time = voltages.shape[3]
    slots = plan.shape[2]
    scale = 1.0 / time
    has_left, has_right = outer > 0, outer < n_out - 1

    barrier = pltpu.get_barrier_semaphore()
    peers = []
    for step in range(1, n_stn * INNER):
        to_stn = lax.rem(stn + step // INNER, n_stn)
        to_inner = lax.rem(inner + step % INNER, INNER)
        peers.append((to_stn, to_inner))
        pl.semaphore_signal(barrier, inc=1, device_id=(to_stn, outer * INNER + to_inner), device_id_type=MESH)

    @pl.when(has_left)
    def _():
        pl.semaphore_signal(barrier, inc=1, device_id=(stn, chan - INNER), device_id_type=MESH)

    @pl.when(has_right)
    def _():
        pl.semaphore_signal(barrier, inc=1, device_id=(stn, chan + INNER), device_id_type=MESH)

    pl.semaphore_wait(barrier, len(peers) + jnp.where(has_left, 1, 0) + jnp.where(has_right, 1, 0))

    def turn(c):
        for dest in range(n_stn * INNER):
            channel = plan[dest // INNER, (c // slots) * INNER + dest % INNER, c % slots]
            for part in range(2):
                packed[dest, c, :, part * time:(part + 1) * time] = voltages[part, channel]
        rows = pl.ds(pl.multiple_of(inner * stations, stations), stations)
        target = full.at[c, stn, outer, rows]
        for to_stn, to_inner in peers:
            pltpu.make_async_remote_copy(
                packed.at[to_stn * INNER + to_inner, c], target, send1.at[c], recv1.at[c],
                device_id=(to_stn, outer * INNER + to_inner), device_id_type=MESH,
            ).start()
        pltpu.make_async_copy(packed.at[stn * INNER + inner, c], target, recv1.at[c]).start()

    def line(c, block, way):
        part = full.at[c, :, block]
        return pltpu.make_async_remote_copy(
            part, part, send2.at[way, block, c], recv2.at[block, c],
            device_id=(stn, chan + (INNER if way else -INNER)), device_id_type=MESH,
        )

    def send(c, block, way):
        @pl.when(c >= WINDOW)
        def _():
            line(c - WINDOW, block, way).wait_send()

        line(c, block, way).start()

    def back(c):
        return pltpu.make_async_remote_copy(
            made.at[c, 1 - inner], own_out.at[inner * count + c], send3.at[c], recv3.at[c],
            device_id=(stn, outer * INNER + 1 - inner), device_id_type=MESH,
        )

    def keep(c):
        return pltpu.make_async_copy(made.at[c, inner], own_out.at[inner * count + c], local3.at[c])

    def correlate(c, half):
        span = INNER * stations
        pieces = n_out // INNER
        left = full[c, outer, pl.ds(half * pieces, pieces)].reshape(pieces * span, -1)
        turned = jnp.concatenate([left[:, time:], -left[:, :time]], axis=1)
        both = jnp.concatenate([left, turned], axis=0)
        for col in range(n_stn):
            right = full[c, col].reshape(n_out * span, -1)
            product = lax.dot_general(both, right, (((1,), (1,)), ((), ())), preferred_element_type=jnp.float32)
            made[c, half, :, :, col * n_out * span:(col + 1) * n_out * span] = (
                (product * scale).astype(jnp.bfloat16).reshape(2, pieces * span, n_out * span)
            )

    for c in range(AHEAD):
        turn(c)

    @pl.loop(0, count + LEAD)
    def _(t):
        @pl.when(t < count - AHEAD)
        def _():
            turn(t + AHEAD)

        @pl.when(t < count)
        def _():
            part = full.at[t, :, outer]
            pltpu.make_async_copy(part, part, recv1.at[t]).wait()

            @pl.when(has_left)
            def _():
                send(t, outer, 0)

            @pl.when(has_right)
            def _():
                send(t, outer, 1)

        c = t - LEAD
        live = c >= 0
        for d in range(1, n_out):

            @pl.when(jnp.logical_and(live, outer - d >= 0))
            def _():
                line(c, outer - d, 1).wait_recv()

                @pl.when(has_right)
                def _():
                    send(c, outer - d, 1)

            @pl.when(jnp.logical_and(live, outer + d < n_out))
            def _():
                line(c, outer + d, 0).wait_recv()

                @pl.when(has_left)
                def _():
                    send(c, outer + d, 0)

        @pl.when(live)
        def _():
            correlate(c, 1 - inner)
            back(c).start()
            correlate(c, inner)
            keep(c).start()

    for k in range(count // n_out):
        total = jnp.zeros((8, full.shape[4]), jnp.float32)
        for a in range(n_stn):
            values = full[outer * (count // n_out) + k, a].astype(jnp.float32)
            total = total + jnp.sum((values * values).reshape(-1, 8, full.shape[4]), axis=0)
        power[0, 0, k] = jnp.sum(total) * scale / (n_stn * n_out * INNER * stations)

    @pl.loop(0, count)
    def _(c):
        part = packed.at[pl.ds(0, n_stn * INNER - 1), c]
        pltpu.make_async_copy(part, part, send1.at[c]).wait()

        @pl.when(c >= count - WINDOW)
        def _():
            for block in range(n_out):
                @pl.when(jnp.logical_and(has_right, outer >= block))
                def _():
                    line(c, block, 1).wait_send()

                @pl.when(jnp.logical_and(has_left, outer <= block))
                def _():
                    line(c, block, 0).wait_send()

        back(c).wait_send()
        back(c).wait_recv()
        keep(c).wait()


def gather_and_correlate(plan, voltages, n_stn, n_out):
    _, _, stations, time = voltages.shape
    count = n_out * plan.shape[2]
    depth = 2 * time
    total_rows = n_stn * n_out * INNER * stations
    rows = total_rows // (n_out * INNER)
    dma = pltpu.SemaphoreType.DMA
    return pl.pallas_call(
        functools.partial(gather_kernel, n_stn, n_out),
        out_shape=(
            pltpu.VMEM((INNER * count, 2, rows, total_rows), jnp.bfloat16),
            jax.ShapeDtypeStruct((1, 1, count // n_out), jnp.float32),
        ),
        in_specs=[pl.BlockSpec(memory_space=pltpu.SMEM), pl.BlockSpec(memory_space=pltpu.VMEM)],
        out_specs=(pl.BlockSpec(memory_space=pl.ANY), pl.BlockSpec(memory_space=pltpu.SMEM)),
        scratch_shapes=[
            pltpu.VMEM((n_stn * INNER, count, stations, depth), jnp.bfloat16),
            pltpu.VMEM((count, n_stn, n_out, INNER * stations, depth), jnp.bfloat16),
            pltpu.VMEM((count, INNER, 2, rows, total_rows), jnp.bfloat16),
            dma((count,)), dma((count,)),
            dma((n_out, count)), dma((2, n_out, count)),
            dma((count,)), dma((count,)), dma((count,)),
        ],
        compiler_params=pltpu.CompilerParams(
            collective_id=0, has_side_effects=True, vmem_limit_bytes=54 * 1024 * 1024
        ),
    )(plan, voltages)


def spread_kernel(plan, flagged, made, out, zeros, write_sem, zero_sem):
    stn = lax.axis_index("stn")
    slots, group_size = made.shape[0], out.shape[0]
    first = stn * group_size
    idle = group_size - slots

    depth = plan.shape[2]
    count = slots // INNER

    def write(j):
        channel = plan[stn, (j % count) // depth * INNER + j // count, j % depth]
        return pltpu.make_async_copy(made.at[j], out.at[channel - first], write_sem.at[j])

    def clear(j):
        return pltpu.make_async_copy(zeros, out.at[flagged[stn * idle + j] - first], zero_sem.at[j])

    for j in range(slots):
        write(j).start()
    zeros[...] = jnp.zeros_like(zeros)
    for j in range(idle):
        clear(j).start()
    for j in range(slots):
        write(j).wait()
    for j in range(idle):
        clear(j).wait()


def spread(plan, flagged, made, group_size):
    slots, idle = made.shape[0], group_size - made.shape[0]
    return pl.pallas_call(
        spread_kernel,
        out_shape=jax.ShapeDtypeStruct((group_size,) + made.shape[1:], made.dtype),
        in_specs=[pl.BlockSpec(memory_space=pltpu.SMEM)] * 2 + [pl.BlockSpec(memory_space=pl.ANY)],
        out_specs=pl.BlockSpec(memory_space=pl.ANY),
        scratch_shapes=[
            pltpu.VMEM(made.shape[1:], made.dtype),
            pltpu.SemaphoreType.DMA((slots,)),
            pltpu.SemaphoreType.DMA((idle,)),
        ],
        compiler_params=pltpu.CompilerParams(vmem_limit_bytes=16 * 1024 * 1024),
    )(plan, flagged, made)


def correlate_gathered(plan, voltages, n_stn, n_out):
    _, _, stations, time = voltages.shape
    count, depth = plan.shape[0] // (n_stn * INNER), 2 * time
    chan_idx = lax.axis_index("chan")
    packed = jnp.take(voltages, plan, axis=1).transpose(1, 2, 0, 3)
    n_chan = n_out * INNER
    shards = packed.reshape(n_stn, INNER * count, stations, depth)
    turned = lax.all_to_all(shards, "stn", split_axis=0, concat_axis=0, tiled=True)
    full = lax.all_gather(turned, "chan", axis=1)
    full = full.transpose(2, 0, 1, 3, 4).reshape(INNER * count, -1, depth)
    total_rows = full.shape[1]
    rows = total_rows // n_chan
    left = lax.dynamic_slice_in_dim(full, chan_idx * rows, rows, 1)
    turned_left = jnp.concatenate([left[..., time:], -left[..., :time]], axis=-1)
    both = jnp.stack([left, turned_left], axis=1)
    made = jnp.einsum("cprk,csk->cprs", both, full, preferred_element_type=jnp.float32) * (1.0 / time)
    slots = count // n_out
    first = (chan_idx % INNER) * count + (chan_idx // INNER) * slots
    own = lax.dynamic_slice_in_dim(full, first, slots, 0).astype(jnp.float32)
    power = jnp.sum(own * own, axis=(1, 2)) * (1.0 / time) / total_rows
    return made.astype(jnp.bfloat16), power.reshape(1, 1, slots)


def on_device(voltages, flagged_ids, work_plan):
    n_stn, n_chan = lax.axis_size("stn"), lax.axis_size("chan")
    n_out = n_chan // INNER
    _, channels, stations, _ = voltages.shape
    slot_count = work_plan.shape[2]
    if n_stn == n_out and stations % 16 == 0:
        made, power = gather_and_correlate(work_plan, voltages, n_stn, n_out)
    else:
        plan = work_plan.reshape(n_stn, n_out, INNER, slot_count).transpose(0, 2, 1, 3).reshape(-1)
        made, power = correlate_gathered(plan, voltages, n_stn, n_out)
    return spread(work_plan, flagged_ids, made, channels // n_stn), power


def solution(mesh):
    in_specs = (P(None, None, ("stn", "chan"), None), P(), P())
    out_specs = (P("stn", None, "chan", None), P("stn", "chan", None))
    return jax.shard_map(
        on_device, mesh=mesh, in_specs=in_specs, out_specs=out_specs, check_vma=False
    )
```

```python
import functools

import jax
import jax.numpy as jnp
from jax import lax
from jax.experimental import pallas as pl
from jax.experimental.pallas import tpu as pltpu
from jax.sharding import PartitionSpec as P

MESH = pl.DeviceIdType.MESH
WINDOW = 2
LEAD = 1
AHEAD = 2
INNER = 2


def gather_kernel(n_stn, n_out, plan, voltages, own_out, power, packed, full, made, recv1, send1, recv2, send2, send3, recv3, local3):
    stn = lax.axis_index("stn")
    chan = lax.axis_index("chan")
    outer, inner = chan // INNER, chan % INNER
    count, stations = packed.shape[1], packed.shape[2]
    time = voltages.shape[3]
    slots = plan.shape[2]
    scale = 1.0 / time
    has_left, has_right = outer > 0, outer < n_out - 1

    barrier = pltpu.get_barrier_semaphore()
    peers = []
    for step in range(1, n_stn * INNER):
        to_stn = lax.rem(stn + step // INNER, n_stn)
        to_inner = lax.rem(inner + step % INNER, INNER)
        peers.append((to_stn, to_inner))
        pl.semaphore_signal(barrier, inc=1, device_id=(to_stn, outer * INNER + to_inner), device_id_type=MESH)

    @pl.when(has_left)
    def _():
        pl.semaphore_signal(barrier, inc=1, device_id=(stn, chan - INNER), device_id_type=MESH)

    @pl.when(has_right)
    def _():
        pl.semaphore_signal(barrier, inc=1, device_id=(stn, chan + INNER), device_id_type=MESH)

    pl.semaphore_wait(barrier, len(peers) + jnp.where(has_left, 1, 0) + jnp.where(has_right, 1, 0))

    def turn(c):
        for dest in range(n_stn * INNER):
            channel = plan[dest // INNER, (c // slots) * INNER + dest % INNER, c % slots]
            for part in range(2):
                packed[dest, c, :, part * time:(part + 1) * time] = voltages[part, channel]
        rows = pl.ds(pl.multiple_of(inner * stations, stations), stations)
        target = full.at[c, stn, outer, rows]
        for to_stn, to_inner in peers:
            pltpu.make_async_remote_copy(
                packed.at[to_stn * INNER + to_inner, c], target, send1.at[c], recv1.at[c],
                device_id=(to_stn, outer * INNER + to_inner), device_id_type=MESH,
            ).start()
        pltpu.make_async_copy(packed.at[stn * INNER + inner, c], target, recv1.at[c]).start()

    def line(c, block, way):
        part = full.at[c, :, block]
        return pltpu.make_async_remote_copy(
            part, part, send2.at[way, block, c], recv2.at[block, c],
            device_id=(stn, chan + (INNER if way else -INNER)), device_id_type=MESH,
        )

    def send(c, block, way):
        @pl.when(c >= WINDOW)
        def _():
            line(c - WINDOW, block, way).wait_send()

        line(c, block, way).start()

    def back(c):
        return pltpu.make_async_remote_copy(
            made.at[c, 1 - inner], own_out.at[inner * count + c], send3.at[c], recv3.at[c],
            device_id=(stn, outer * INNER + 1 - inner), device_id_type=MESH,
        )

    def keep(c):
        return pltpu.make_async_copy(made.at[c, inner], own_out.at[inner * count + c], local3.at[c])

    def correlate(c, half):
        span = INNER * stations
        pieces = n_out // INNER
        left = full[c, outer, pl.ds(half * pieces, pieces)].reshape(pieces * span, -1)
        turned = jnp.concatenate([left[:, time:], -left[:, :time]], axis=1)
        both = jnp.concatenate([left, turned], axis=0)
        for col in range(n_stn):
            right = full[c, col].reshape(n_out * span, -1)
            product = lax.dot_general(both, right, (((1,), (1,)), ((), ())), preferred_element_type=jnp.float32)
            made[c, half, :, :, col * n_out * span:(col + 1) * n_out * span] = (
                (product * scale).astype(jnp.bfloat16).reshape(2, pieces * span, n_out * span)
            )

    for c in range(AHEAD):
        turn(c)

    @pl.loop(0, count + LEAD)
    def _(t):
        @pl.when(t < count - AHEAD)
        def _():
            turn(t + AHEAD)

        @pl.when(t < count)
        def _():
            part = full.at[t, :, outer]
            pltpu.make_async_copy(part, part, recv1.at[t]).wait()

            @pl.when(has_left)
            def _():
                send(t, outer, 0)

            @pl.when(has_right)
            def _():
                send(t, outer, 1)

        c = t - LEAD
        live = c >= 0
        for d in range(1, n_out):

            @pl.when(jnp.logical_and(live, outer - d >= 0))
            def _():
                line(c, outer - d, 1).wait_recv()

                @pl.when(has_right)
                def _():
                    send(c, outer - d, 1)

            @pl.when(jnp.logical_and(live, outer + d < n_out))
            def _():
                line(c, outer + d, 0).wait_recv()

                @pl.when(has_left)
                def _():
                    send(c, outer + d, 0)

        @pl.when(live)
        def _():
            correlate(c, 1 - inner)
            back(c).start()
            correlate(c, inner)
            keep(c).start()

    for k in range(count // n_out):
        total = jnp.zeros((8, full.shape[4]), jnp.float32)
        for a in range(n_stn):
            values = full[outer * (count // n_out) + k, a].astype(jnp.float32)
            total = total + jnp.sum((values * values).reshape(-1, 8, full.shape[4]), axis=0)
        power[0, 0, k] = jnp.sum(total) * scale / (n_stn * n_out * INNER * stations)

    @pl.loop(0, count)
    def _(c):
        part = packed.at[pl.ds(0, n_stn * INNER - 1), c]
        pltpu.make_async_copy(part, part, send1.at[c]).wait()

        @pl.when(c >= count - WINDOW)
        def _():
            for block in range(n_out):
                @pl.when(jnp.logical_and(has_right, outer >= block))
                def _():
                    line(c, block, 1).wait_send()

                @pl.when(jnp.logical_and(has_left, outer <= block))
                def _():
                    line(c, block, 0).wait_send()

        back(c).wait_send()
        back(c).wait_recv()
        keep(c).wait()


def gather_and_correlate(plan, voltages, n_stn, n_out):
    _, _, stations, time = voltages.shape
    count = n_out * plan.shape[2]
    depth = 2 * time
    total_rows = n_stn * n_out * INNER * stations
    rows = total_rows // (n_out * INNER)
    dma = pltpu.SemaphoreType.DMA
    return pl.pallas_call(
        functools.partial(gather_kernel, n_stn, n_out),
        out_shape=(
            pltpu.VMEM((INNER * count, 2, rows, total_rows), jnp.bfloat16),
            jax.ShapeDtypeStruct((1, 1, count // n_out), jnp.float32),
        ),
        in_specs=[pl.BlockSpec(memory_space=pltpu.SMEM), pl.BlockSpec(memory_space=pltpu.VMEM)],
        out_specs=(pl.BlockSpec(memory_space=pl.ANY), pl.BlockSpec(memory_space=pltpu.SMEM)),
        scratch_shapes=[
            pltpu.VMEM((n_stn * INNER, count, stations, depth), jnp.bfloat16),
            pltpu.VMEM((count, n_stn, n_out, INNER * stations, depth), jnp.bfloat16),
            pltpu.VMEM((count, INNER, 2, rows, total_rows), jnp.bfloat16),
            dma((count,)), dma((count,)),
            dma((n_out, count)), dma((2, n_out, count)),
            dma((count,)), dma((count,)), dma((count,)),
        ],
        compiler_params=pltpu.CompilerParams(
            collective_id=0, has_side_effects=True, vmem_limit_bytes=30 * 1024 * 1024
        ),
    )(plan, voltages)


def spread_kernel(plan, flagged, made, out, zeros, write_sem, zero_sem):
    stn = lax.axis_index("stn")
    slots, group_size = made.shape[0], out.shape[0]
    first = stn * group_size
    idle = group_size - slots

    depth = plan.shape[2]
    count = slots // INNER

    def write(j):
        channel = plan[stn, (j % count) // depth * INNER + j // count, j % depth]
        return pltpu.make_async_copy(made.at[j], out.at[channel - first], write_sem.at[j])

    def clear(j):
        return pltpu.make_async_copy(zeros, out.at[flagged[stn * idle + j] - first], zero_sem.at[j])

    for j in range(slots):
        write(j).start()
    zeros[...] = jnp.zeros_like(zeros)
    for j in range(idle):
        clear(j).start()
    for j in range(slots):
        write(j).wait()
    for j in range(idle):
        clear(j).wait()


def spread(plan, flagged, made, group_size):
    slots, idle = made.shape[0], group_size - made.shape[0]
    return pl.pallas_call(
        spread_kernel,
        out_shape=jax.ShapeDtypeStruct((group_size,) + made.shape[1:], made.dtype),
        in_specs=[pl.BlockSpec(memory_space=pltpu.SMEM)] * 2 + [pl.BlockSpec(memory_space=pl.ANY)],
        out_specs=pl.BlockSpec(memory_space=pl.ANY),
        scratch_shapes=[
            pltpu.VMEM(made.shape[1:], made.dtype),
            pltpu.SemaphoreType.DMA((slots,)),
            pltpu.SemaphoreType.DMA((idle,)),
        ],
        compiler_params=pltpu.CompilerParams(vmem_limit_bytes=16 * 1024 * 1024),
    )(plan, flagged, made)


def correlate_gathered(plan, voltages, n_stn, n_out):
    _, _, stations, time = voltages.shape
    count, depth = plan.shape[0] // (n_stn * INNER), 2 * time
    chan_idx = lax.axis_index("chan")
    packed = jnp.take(voltages, plan, axis=1).transpose(1, 2, 0, 3)
    n_chan = n_out * INNER
    shards = packed.reshape(n_stn, INNER * count, stations, depth)
    turned = lax.all_to_all(shards, "stn", split_axis=0, concat_axis=0, tiled=True)
    full = lax.all_gather(turned, "chan", axis=1)
    full = full.transpose(2, 0, 1, 3, 4).reshape(INNER * count, -1, depth)
    total_rows = full.shape[1]
    rows = total_rows // n_chan
    left = lax.dynamic_slice_in_dim(full, chan_idx * rows, rows, 1)
    turned_left = jnp.concatenate([left[..., time:], -left[..., :time]], axis=-1)
    both = jnp.stack([left, turned_left], axis=1)
    made = jnp.einsum("cprk,csk->cprs", both, full, preferred_element_type=jnp.float32) * (1.0 / time)
    slots = count // n_out
    first = (chan_idx % INNER) * count + (chan_idx // INNER) * slots
    own = lax.dynamic_slice_in_dim(full, first, slots, 0).astype(jnp.float32)
    power = jnp.sum(own * own, axis=(1, 2)) * (1.0 / time) / total_rows
    return made.astype(jnp.bfloat16), power.reshape(1, 1, slots)


def on_device(voltages, flagged_ids, work_plan):
    n_stn, n_chan = lax.axis_size("stn"), lax.axis_size("chan")
    n_out = n_chan // INNER
    _, channels, stations, _ = voltages.shape
    slot_count = work_plan.shape[2]
    if n_stn == n_out and stations % 16 == 0:
        made, power = gather_and_correlate(work_plan, voltages, n_stn, n_out)
    else:
        plan = work_plan.reshape(n_stn, n_out, INNER, slot_count).transpose(0, 2, 1, 3).reshape(-1)
        made, power = correlate_gathered(plan, voltages, n_stn, n_out)
    return spread(work_plan, flagged_ids, made, channels // n_stn), power


def solution(mesh):
    in_specs = (P(None, None, ("stn", "chan"), None), P(), P())
    out_specs = (P("stn", None, "chan", None), P("stn", "chan", None))
    return jax.shard_map(
        on_device, mesh=mesh, in_specs=in_specs, out_specs=out_specs, check_vma=False
    )
```
